256 devices in a mesh: cls: 32 (over z, x), pb: 8 (over y, core).
Axes of the slice: x: 4, y: 4, z: 8, core: 2. Of those that a mesh axis runs over, the one named last changes fastest.
Arguments:
- queries: bfloat16 [4096, 1024], P('pb'), may hold values from -40 to 40
- labels: int32 [4096], replicated, may hold values from 0 to 98303
- prototypes: bfloat16 [98304, 1024], P('cls'), may hold values from -8 to 8
Outputs:
- query_loss: float32 [4096], P('pb')
- query_grad: float32 [4096, 1024], P('pb')
- proto_grad: float32 [98304, 1024], P(('cls', 'pb'))
The draws below stay inside these ranges and needn't reach their ends.
All inputs are finite; a program needn't handle non-finite values.
Results may differ from the reference program's by a relative error of at most 0.0012.
Values may be sent and summed in bfloat16 or wider, within the bound.
A program may use at most 128 MiB of HBM per device.

```python
import math
import jax
import jax.numpy as jnp
from jax import lax

D = 1024
CLS_DEV = 3072
B = 4096
CLASSES = 98304
N_CLS = 32


def proto_table(key):
    table = jax.random.truncated_normal(jax.random.fold_in(key, 7), -6.0, 6.0, (CLASSES, D), jnp.float32)
    return table


def draw_prototypes(key, part):
    return proto_table(key).astype(jnp.bfloat16)


def draw_queries(key, part):
    fresh = jax.random.truncated_normal(jax.random.fold_in(key, 11), -6.0, 6.0, (B, D), jnp.float32)
    return fresh.astype(jnp.bfloat16)


def with_ends(values, own_key, low, largest):
    index_at = [jax.random.randint(jax.random.fold_in(own_key, axis), (), 0, length) for axis, length in enumerate(values.shape)]
    longest = values.shape.index(max(values.shape))
    next_to = index_at[:longest] + [(index_at[longest] + 1) % values.shape[longest]] + index_at[longest + 1:]
    return values.at[tuple(index_at)].set(low).at[tuple(next_to)].set(largest)


def setup_inputs(seed: int = 0) -> dict:
    key_list = jax.random.split(jax.random.key(seed), 4)
    return {
        "queries": draw_queries(jax.random.fold_in(key_list[3], 71), 0),
        "labels": with_ends(jax.random.randint(key_list[1], (B,), 0, CLASSES), jax.random.fold_in(key_list[1], 1), 0, CLASSES - 1).astype(jnp.int32),
        "prototypes": draw_prototypes(jax.random.fold_in(key_list[3], 71), 0),
    }


def block_logits(queries, query_norm, proto_block, factor):
    inner_block = jnp.dot(queries, proto_block.T, preferred_element_type=jnp.float32)
    proto_float = proto_block.astype(jnp.float32)
    proto_norm = lax.optimization_barrier(jnp.sum(proto_float * proto_float, axis=1))
    return factor * (2.0 * inner_block - proto_norm[None, :] - query_norm[:, None])

def reference(queries, labels, prototypes):
    factor = 1.0 / math.sqrt(D)
    query_float = queries.astype(jnp.float32)
    query_norm = lax.optimization_barrier(jnp.sum(query_float * query_float, axis=1))
    blocks = prototypes.reshape(N_CLS, CLS_DEV, D)
    indices = jnp.arange(N_CLS, dtype=jnp.int32)

    def first_pass(state, item):
        row_top, row_total, label_logit = state
        index_k, proto_block = item
        logit_block = block_logits(queries, query_norm, proto_block, factor)
        columns = index_k * CLS_DEV + jnp.arange(CLS_DEV, dtype=jnp.int32)
        label_mask = labels[:, None] == columns[None, :]
        new_top = jnp.maximum(row_top, lax.optimization_barrier(jnp.max(logit_block, axis=1)))
        row_total = row_total * jnp.exp(row_top - new_top) + lax.optimization_barrier(jnp.sum(jnp.exp(logit_block - new_top[:, None]), axis=1))
        label_logit = label_logit + lax.optimization_barrier(jnp.sum(jnp.where(label_mask, logit_block, 0.0), axis=1))
        return ((new_top, row_total, label_logit), None)
    start_state = (jnp.full((B,), -jnp.inf, jnp.float32), jnp.zeros((B,), jnp.float32), jnp.zeros((B,), jnp.float32))
    (row_top, row_total, label_logit), _ = lax.scan(first_pass, start_state, (indices, blocks))
    log_total = row_top + jnp.log(row_total)
    query_loss = log_total - label_logit

    def second_pass(query_sum, item):
        index_k, proto_block = item
        logit_block = block_logits(queries, query_norm, proto_block, factor)
        columns = index_k * CLS_DEV + jnp.arange(CLS_DEV, dtype=jnp.int32)
        label_mask = (labels[:, None] == columns[None, :]).astype(jnp.float32)
        grad_logit = (jnp.exp(logit_block - log_total[:, None]) - label_mask).astype(jnp.bfloat16)
        query_sum = query_sum + jnp.dot(grad_logit, proto_block, preferred_element_type=jnp.float32)
        col_total = lax.optimization_barrier(jnp.sum(grad_logit.astype(jnp.float32), axis=0))
        moment = jnp.dot(grad_logit.T, queries, preferred_element_type=jnp.float32)
        proto_part = 2.0 * factor * (moment - col_total[:, None] * proto_block.astype(jnp.float32))
        return (query_sum, proto_part)
    query_sum, proto_parts = lax.scan(second_pass, jnp.zeros((B, D), jnp.float32), (indices, blocks))
    query_grad = 2.0 * factor * query_sum
    proto_grad = proto_parts.reshape(CLASSES, D)
    return (query_loss, query_grad, proto_grad)
```

```python
import math

import jax
import jax.numpy as jnp
from jax import lax
from jax.experimental import pallas as pl
from jax.experimental.pallas import tpu as pltpu
from jax.sharding import PartitionSpec as P

MESH = pl.DeviceIdType.MESH
NX, NZ, NY = 4, 8, 4
PARTS = 2
TOP = 32000.0

NT = (((1,), (1,)), ((), ()))
NN = (((1,), (0,)), ((), ()))
SLOTS = ((0, 0), (0, 1), (3, 0), (1, 0), (3, 1), (1, 1), (2, 0), (2, 1))


def dot(a, b, dims):
    return lax.dot_general(a, b, dims, preferred_element_type=jnp.float32)


def coded(value):
    top = jnp.max(jnp.abs(value), axis=0, keepdims=True)
    power = jnp.ceil(jnp.log2(jnp.maximum(top, 1e-30)) + 1e-4)
    lines = jnp.round(value * (jnp.exp2(-power) * TOP))
    lines = jnp.clip(lines, -32767.0, 32767.0)
    lines = lines.astype(jnp.int32).astype(jnp.int16)
    return lines, jnp.broadcast_to(power, (16, power.shape[1])).astype(jnp.int32).astype(jnp.int16)


def scale_of(power):
    return jnp.exp2(power.astype(jnp.float32)) * (1.0 / TOP)


def lanes_of(tile, first):
    return jnp.concatenate([tile[first + k : first + k + 1] for k in range(4)], axis=1)


def rows_of(line):
    return jnp.concatenate([line[:, 128 * k : 128 * k + 128] for k in range(4)], axis=0)


def kernel(
    q_in, labels, p_in, loss_out, qg_out, pg_out,
    protos, qall, logits, grad, pn_line, own_x, stat_x, stat_z, row_line,
    lab_col, m_col, tot_col, lbl_col, w_col,
    xs, xr, zs, zr, zown, gx, acc, coltot, pn_own,
    in_sem, q_ssem, q_rsem, st_ssem, st_rsem, pb_ssem, pb_rsem,
    x_ssem, x_rsem, z_ssem, z_rsem, gz_ssem, gz_rsem, gx_ssem, gx_rsem,
):
    ci, pi = lax.axis_index("cls"), lax.axis_index("pb")
    z, x, y, core = ci // NX, lax.rem(ci, NX), pi // 2, lax.rem(pi, 2)
    queries, width = q_in.shape
    classes = p_in.shape[0]
    own_rows = pg_out.shape[0]
    factor = 1.0 / math.sqrt(width)
    block = queries // NX
    part = block // PARTS
    first_class = ci * classes

    def at_x(d):
        return lax.rem(x + d, NX)

    def at_z(d):
        return lax.rem(z + d, NZ)

    def dev_x(d):
        return (z * NX + at_x(d), pi)

    def dev_z(d):
        return (at_z(d) * NX + x, pi)

    def dev_pb(dy, other):
        return (ci, lax.rem(y + dy, NY) * 2 + lax.rem(core + other, 2))

    def pb_of(slot):
        dy, other = SLOTS[slot]
        return lax.rem(y + dy, NY) * 2 + lax.rem(core + other, 2)

    def send(src, dst, ssem, rsem, dev):
        copy = pltpu.make_async_remote_copy(
            src_ref=src, dst_ref=dst, send_sem=ssem, recv_sem=rsem, device_id=dev, device_id_type=MESH
        )
        copy.start()
        return copy

    def arrived(ref, ssem, rsem):
        pltpu.make_async_remote_copy(
            src_ref=ref, dst_ref=ref, send_sem=ssem, recv_sem=rsem, device_id=(ci, pi), device_id_type=MESH
        ).wait_recv()

    sent = []

    chunk = 512
    chunks = classes // chunk
    q_load = pltpu.make_async_copy(q_in, qall.at[0], in_sem.at[chunks])
    q_load.start()
    p_loads = [
        pltpu.make_async_copy(p_in.at[pl.ds(k * chunk, chunk)], protos.at[pl.ds(k * chunk, chunk)], in_sem.at[k])
        for k in range(chunks)
    ]
    for load in p_loads:
        load.start()

    barrier = pltpu.get_barrier_semaphore()
    peers = [dev_x(d) for d in range(1, NX)] + [dev_z(d) for d in range(1, NZ)]
    peers += [dev_pb(dy, o) for dy in range(NY) for o in range(2) if dy or o]
    for dev in peers:
        pl.semaphore_signal(barrier, inc=1, device_id=dev, device_id_type=MESH)

    q_load.wait()
    my_label = lanes_of(labels[pi], 0)
    lab_col[...] = jnp.broadcast_to(my_label - first_class, (128, queries)).T

    for k in range(queries // 128):
        q32 = qall[0, pl.ds(k * 128, 128), :].astype(jnp.float32)
        q32 = q32 * q32
        part_sum = sum(q32[:, 128 * i : 128 * i + 128] for i in range(width // 128))
        row_line[1:2, 128 * k : 128 * k + 128] = factor * jnp.sum(part_sum.T, axis=0, keepdims=True)

    for k in range(chunks):
        p_loads[k].wait()

    @pl.loop(0, chunks)
    def _(k):
        base = pl.multiple_of(k * chunk, chunk)
        for i in range(chunk // 128):
            p32 = protos[pl.ds(base + i * 128, 128), :].astype(jnp.float32)
            p32 = p32 * p32
            part_sum = sum(p32[:, 128 * n : 128 * n + 128] for n in range(width // 128))
            pn_line[0:1, pl.ds(base + i * 128, 128)] = factor * jnp.sum(part_sum.T, axis=0, keepdims=True)
        for i in range(chunk // 256):
            at = pl.ds(pl.multiple_of(base + i * 256, 256), 256)
            inner = dot(qall[0], protos[at, :], NT)
            logits[:, at] = inner * (2.0 * factor) - pn_line[0:1, at]

    pl.semaphore_wait(barrier, len(peers))

    half = queries // 2
    halves = (pl.ds(0, half), pl.ds(half, half))
    slot_at = {s: n for n, s in enumerate(SLOTS)}
    up, down = dev_pb(1, 0), dev_pb(NY - 1, 0)
    sibling = dev_pb(0, 1)

    def q_send(src_slot, dst_slot, rows, n, dev):
        sent.append(
            send(qall.at[src_slot, rows], qall.at[dst_slot, rows], q_ssem.at[n], q_rsem.at[n], dev)
        )

    q_send(0, slot_at[3, 0], halves[0], 0, up)
    q_send(0, slot_at[1, 0], halves[1], 2, down)
    q_send(0, slot_at[0, 1], halves[0], 6, sibling)
    q_send(0, slot_at[0, 1], halves[1], 7, sibling)
    q_send(0, slot_at[3, 0], halves[1], 1, up)
    q_send(0, slot_at[1, 0], halves[0], 3, down)

    def q_wait(slot, rows, n):
        arrived(qall.at[slot, rows], q_ssem.at[n], q_rsem.at[n])

    lane = lax.broadcasted_iota(jnp.int32, (16, 128), 1)

    @pl.loop(0, queries // 16)
    def _(r):
        rows = pl.ds(pl.multiple_of(r * 16, 16), 16)
        tiles = [logits[rows, 128 * k : 128 * k + 128] for k in range(classes // 128)]
        top = tiles[0]
        for t in tiles[1:]:
            top = jnp.maximum(top, t)
        top = jnp.broadcast_to(jnp.max(top, axis=1, keepdims=True), (16, 128))
        label = lab_col[rows, :] - lane
        total = jnp.zeros((16, 128), jnp.float32)
        mine = jnp.zeros((16, 128), jnp.float32)
        for k, t in enumerate(tiles):
            mine = mine + jnp.where(label == 128 * k, t, 0.0)
            e = jnp.exp(t - top)
            total = total + e
            logits[rows, 128 * k : 128 * k + 128] = e
        m_col[rows, :] = top
        tot_col[rows, :] = total
        lbl_col[rows, :] = mine

    q_line = row_line[1:2, :]
    m_line = m_col[...].T[0:1] - q_line
    t_line = jnp.sum(tot_col[...].T, axis=0, keepdims=True)
    l_line = jnp.sum(lbl_col[...].T, axis=0, keepdims=True)
    has = jnp.logical_and(my_label >= first_class, my_label < first_class + classes)
    l_line = jnp.where(has, l_line - q_line, 0.0)
    stat_x[x] = jnp.concatenate([rows_of(m_line + jnp.log(t_line)), rows_of(l_line)], axis=0)

    upper = lax.broadcasted_iota(jnp.int32, (8, 128), 0) < 4

    def combined(tiles):
        top = tiles[0]
        for t in tiles[1:]:
            top = jnp.maximum(top, t)
        total = sum(jnp.exp(t - top) for t in tiles)
        return jnp.where(upper, top + jnp.log(total), sum(tiles))

    for d in (2, 1, 3):
        sent.append(send(stat_x.at[x], stat_x.at[x], st_ssem.at[d], st_rsem.at[x], dev_x(d)))
    for d in (1, 3, 2):
        arrived(stat_x.at[at_x(d)], st_ssem.at[0], st_rsem.at[at_x(d)])
    stat_z[z] = combined([stat_x[k] for k in range(NX)])
    for d in (4, 3, 5, 2, 6, 1, 7):
        sent.append(send(stat_z.at[z], stat_z.at[z], st_ssem.at[NX + d], st_rsem.at[NX + z], dev_z(d)))
    for d in (1, 7, 2, 6, 3, 5, 4):
        arrived(stat_z.at[at_z(d)], st_ssem.at[0], st_rsem.at[NX + at_z(d)])
    stats = combined([stat_z[k] for k in range(NZ)])
    log_total = lanes_of(stats, 0)
    loss_out[...] = stats[0:4] - stats[4:8]

    mine_line = log_total + q_line
    row_line[pl.ds(0, 1), :] = mine_line
    qb = jnp.concatenate([rows_of(mine_line), rows_of(mine_line)], axis=0)
    stat_x[NX] = qb
    for s in range(1, 8):
        dy, other = SLOTS[s]
        dst = slot_at[(NY - dy) % NY, other]
        sent.append(
            send(stat_x.at[NX], stat_x.at[NX + dst], pb_ssem.at[s], pb_rsem.at[dst], dev_pb(dy, other))
        )

    w_col[...] = jnp.broadcast_to(jnp.exp(m_line - log_total), (128, queries)).T

    def grad_rows(r):
        rows = pl.ds(pl.multiple_of(r * 16, 16), 16)
        label = lab_col[rows, :] - lane
        w = w_col[rows, :]
        for k in range(classes // 128):
            g = logits[rows, 128 * k : 128 * k + 128] * w
            g = g - jnp.where(label == 128 * k, 1.0, 0.0)
            grad[rows, 128 * k : 128 * k + 128] = g.astype(jnp.bfloat16)

    for d in (1, 3, 2, 0):
        at = pl.multiple_of(at_x(d) * block, block)

        @pl.loop(0, block // 16)
        def _(r):
            grad_rows(at_x(d) * (block // 16) + r)

        @pl.loop(0, width // 256)
        def _(n):
            cols = pl.ds(pl.multiple_of(n * 256, 256), 256)
            v = dot(grad[pl.ds(at, block), :], protos[:, cols], NN)
            if d:
                for h in range(PARTS):
                    lines, power = coded(v[h * part : (h + 1) * part])
                    xs[d - 1, h, 0:part, cols] = lines
                    xs[d - 1, h, part : part + 16, cols] = power
            else:
                own_x[:, cols] = v

        if d:
            sent.append(send(xs.at[d - 1, 0], xr.at[d - 1, 0], x_ssem.at[d - 1, 0], x_rsem.at[d - 1, 0], dev_x(d)))
    for h in range(1, PARTS):
        for d in (1, 3, 2):
            sent.append(send(xs.at[d - 1, h], xr.at[d - 1, h], x_ssem.at[d - 1, h], x_rsem.at[d - 1, h], dev_x(d)))

    own_at = pl.multiple_of(pi * own_rows, own_rows)
    for i in range(own_rows // 128):
        p32 = protos[pl.ds(own_at + i * 128, 128), :].astype(jnp.float32)
        p32 = p32 * p32
        part_sum = sum(p32[:, 128 * n : 128 * n + 128] for n in range(width // 128))
        total = jnp.sum(part_sum, axis=1, keepdims=True) * factor
        pn_own[pl.ds(i * 128, 128), :] = jnp.broadcast_to(total, (128, 128))

    def proto_block(slot, first):
        pb = pb_of(slot)
        if slot:
            arrived(stat_x.at[NX + slot], pb_ssem.at[slot], pb_rsem.at[slot])
        term = lanes_of(stat_x[NX + slot], 0)
        label = lanes_of(labels[pb], 0) - first_class - own_at

        @pl.loop(0, own_rows // 128)
        def _(i):
            rows = pl.ds(pl.multiple_of(i * 128, 128), 128)
            inner = dot(protos[pl.ds(pl.multiple_of(own_at + i * 128, 128), 128), :], qall[slot], NT)
            pn = pn_own[rows, :]
            pn = jnp.concatenate([pn] * (queries // 128), axis=1)
            g = jnp.exp(inner * (2.0 * factor) - pn - term)
            index = lax.broadcasted_iota(jnp.int32, (128, queries), 0) + i * 128
            g = (g - jnp.where(index == label, 1.0, 0.0)).astype(jnp.bfloat16)
            g32 = g.astype(jnp.float32)
            col = sum(g32[:, 128 * n : 128 * n + 128] for n in range(queries // 128))
            for n in range(width // 512):
                cols = slice(512 * n, 512 * n + 512)
                moment = dot(g, qall[slot, :, cols], NN)
                if first:
                    acc[rows, cols] = moment
                else:
                    acc[rows, cols] += moment
            if first:
                coltot[rows, :] = col
            else:
                coltot[rows, :] += col

    def x_done(h):
        for d in (1, 3, 2):
            arrived(xr.at[d - 1, h], x_ssem.at[d - 1, h], x_rsem.at[d - 1, h])
        for n in range(NZ):
            cols = slice(128 * n, 128 * n + 128)
            v = own_x[h * part : (h + 1) * part, cols]
            for d in range(1, NX):
                s = scale_of(xr[d - 1, h, part : part + 16, cols])[0:1]
                v = v + xr[d - 1, h, 0:part, cols].astype(jnp.float32) * s
            own_x[h * part : (h + 1) * part, cols] = v
            lines, power = coded(v)
            zs[h, n, 0:part, :] = lines
            zs[h, n, part : part + 16, :] = power
        for d in (4, 3, 5, 2, 6, 1, 7):
            sent.append(
                send(zs.at[h, at_z(d)], zr.at[h, d], z_ssem.at[h, d], z_rsem.at[h, d], dev_z(d))
            )

    def z_done(h):
        for d in (1, 7, 2, 6, 3, 5, 4):
            arrived(zr.at[h, d], z_ssem.at[h, d], z_rsem.at[h, d])
        v = own_x[h * part : (h + 1) * part, pl.ds(pl.multiple_of(z * 128, 128), 128)]
        for d in range(1, NZ):
            s = scale_of(zr[h, d, part : part + 16, :])[0:1]
            v = v + zr[h, d, 0:part, :].astype(jnp.float32) * s
        lines, power = coded(v * (2.0 * factor))
        gx[h, x, z, 0:part, :] = lines
        gx[h, x, z, part : part + 16, :] = power
        for d in (4, 3, 5, 2, 6, 1, 7):
            sent.append(
                send(gx.at[h, x, z], gx.at[h, x, z], gz_ssem.at[h, d], gz_rsem.at[h, z], dev_z(d))
            )

    def gz_done(h):
        for d in (1, 7, 2, 6, 3, 5, 4):
            arrived(gx.at[h, x, at_z(d)], gz_ssem.at[h, d], gz_rsem.at[h, at_z(d)])
        for d in (2, 1, 3):
            sent.append(send(gx.at[h, x], gx.at[h, x], gx_ssem.at[h, d], gx_rsem.at[h, x], dev_x(d)))

    def write_rows(h, xq):
        at = pl.ds(pl.multiple_of(xq * block + h * part, part), part)
        for n in range(NZ):
            s = scale_of(gx[h, xq, n, part : part + 16, :])[0:1]
            qg_out[at, 128 * n : 128 * n + 128] = gx[h, xq, n, 0:part, :].astype(jnp.float32) * s

    def to_other_core(slot, first):
        dy = SLOTS[slot][0]
        for k in range(2):
            q_send(slot, slot_at[dy, 1], halves[k], first + k, sibling)

    def relay():
        q_wait(slot_at[3, 0], halves[0], 0)
        q_send(slot_at[3, 0], slot_at[2, 0], halves[0], 4, up)
        q_wait(slot_at[1, 0], halves[1], 2)
        q_send(slot_at[1, 0], slot_at[2, 0], halves[1], 5, down)

    proto_block(0, True)
    q_wait(slot_at[0, 1], halves[0], 6)
    q_wait(slot_at[0, 1], halves[1], 7)
    proto_block(1, False)
    relay()
    x_done(0)
    x_done(1)
    z_done(0)
    z_done(1)
    q_wait(slot_at[3, 0], halves[1], 1)
    to_other_core(2, 8)
    q_wait(slot_at[1, 0], halves[0], 3)
    to_other_core(3, 10)
    gz_done(0)
    gz_done(1)
    proto_block(2, False)
    proto_block(3, False)
    for k in range(2):
        q_wait(slot_at[3, 1], halves[k], 8 + k)
    proto_block(4, False)
    for k in range(2):
        q_wait(slot_at[1, 1], halves[k], 10 + k)
    proto_block(5, False)
    q_wait(slot_at[2, 0], halves[0], 4)
    q_wait(slot_at[2, 0], halves[1], 5)
    to_other_core(6, 12)
    proto_block(6, False)
    for k in range(2):
        q_wait(slot_at[2, 1], halves[k], 12 + k)
    proto_block(7, False)

    @pl.loop(0, own_rows // 128)
    def _(i):
        rows = pl.ds(pl.multiple_of(i * 128, 128), 128)
        own = protos[pl.ds(pl.multiple_of(own_at + i * 128, 128), 128), :].astype(jnp.float32)
        total = jnp.sum(coltot[rows, :], axis=1, keepdims=True)
        pg_out[rows, :] = (2.0 * factor) * (acc[rows, :] - total * own)

    for h in range(PARTS):
        write_rows(h, x)
    for h in range(PARTS):
        for d in (1, 3, 2):
            arrived(gx.at[h, at_x(d)], gx_ssem.at[h, d], gx_rsem.at[h, at_x(d)])
            write_rows(h, at_x(d))
    for copy in sent:
        copy.wait_send()


def local(queries, labels, prototypes):
    rows, width = queries.shape
    classes = prototypes.shape[0]
    own_rows = classes // (2 * NY)
    block = rows // NX
    part = block // PARTS
    vmem = pltpu.VMEM
    dma = pltpu.SemaphoreType.DMA
    f32, bf16, i16 = jnp.float32, jnp.bfloat16, jnp.int16
    scratch = [
        vmem((classes, width), bf16),
        vmem((2 * NY, rows, width), bf16),
        vmem((rows, classes), f32),
        vmem((rows, classes), bf16),
        vmem((8, classes), f32),
        vmem((block, width), f32),
        vmem((NX + 8, 8, 128), f32),
        vmem((NZ, 8, 128), f32),
        vmem((8, rows), f32),
        vmem((rows, 128), jnp.int32),
        vmem((rows, 128), f32),
        vmem((rows, 128), f32),
        vmem((rows, 128), f32),
        vmem((rows, 128), f32),
        vmem((NX - 1, PARTS, part + 16, width), i16),
        vmem((NX - 1, PARTS, part + 16, width), i16),
        vmem((PARTS, NZ, part + 16, 128), i16),
        vmem((PARTS, NZ, part + 16, 128), i16),
        vmem((part, 128), f32),
        vmem((PARTS, NX, NZ, part + 16, 128), i16),
        vmem((own_rows, width), f32),
        vmem((own_rows, 128), f32),
        vmem((own_rows, 128), f32),
        dma((classes // 512 + 1,)),
        dma((14,)), dma((14,)),
        dma((NX + NZ,)), dma((NX + NZ,)),
        dma((8,)), dma((8,)),
        dma((NX - 1, PARTS)), dma((NX - 1, PARTS)),
        dma((PARTS, NZ)), dma((PARTS, NZ)),
        dma((PARTS, NZ)), dma((PARTS, NZ)),
        dma((PARTS, NX)), dma((PARTS, NX)),
    ]
    loss, query_grad, proto_grad = pl.pallas_call(
        kernel,
        out_shape=(
            jax.ShapeDtypeStruct((4, rows // 4), f32),
            jax.ShapeDtypeStruct((rows, width), f32),
            jax.ShapeDtypeStruct((own_rows, width), f32),
        ),
        in_specs=[
            pl.BlockSpec(memory_space=pl.ANY),
            pl.BlockSpec(memory_space=pltpu.VMEM),
            pl.BlockSpec(memory_space=pl.ANY),
        ],
        out_specs=[pl.BlockSpec(memory_space=pltpu.VMEM)] * 3,
        scratch_shapes=scratch,
        compiler_params=pltpu.CompilerParams(
            collective_id=0, has_side_effects=True, vmem_limit_bytes=60 * 2**20
        ),
    )(queries, labels.reshape(2 * NY, 4, rows // 4), prototypes)
    return loss.reshape(rows), query_grad, proto_grad


def solution(mesh):
    placed = (P("pb", None), P(), P("cls", None))
    return jax.shard_map(
        local,
        mesh=mesh,
        in_specs=placed,
        out_specs=(P("pb"), P("pb", None), P(("cls", "pb"), None)),
        check_vma=False,
    )
```

```python
import math

import jax
import jax.numpy as jnp
from jax import lax
from jax.experimental import pallas as pl
from jax.experimental.pallas import tpu as pltpu
from jax.sharding import PartitionSpec as P

MESH = pl.DeviceIdType.MESH
NX, NZ, NY = 4, 8, 4
PARTS = 2
TOP = 32000.0

NT = (((1,), (1,)), ((), ()))
NN = (((1,), (0,)), ((), ()))
SLOTS = ((0, 0), (0, 1), (3, 0), (1, 0), (3, 1), (1, 1), (2, 0), (2, 1))


def dot(a, b, dims):
    return lax.dot_general(a, b, dims, preferred_element_type=jnp.float32)


def coded(value):
    top = jnp.max(jnp.abs(value), axis=0, keepdims=True)
    power = jnp.ceil(jnp.log2(jnp.maximum(top, 1e-30)) + 1e-4)
    lines = jnp.round(value * (jnp.exp2(-power) * TOP))
    lines = jnp.clip(lines, -32767.0, 32767.0)
    return power, lines.astype(jnp.int32).astype(jnp.int16)


def rows16(power):
    return jnp.broadcast_to(power, (16, power.shape[1])).astype(jnp.int32).astype(jnp.int16)


def scale_of(power):
    return jnp.exp2(power.astype(jnp.float32)) * (1.0 / TOP)


def lanes_of(tile, first):
    return jnp.concatenate([tile[first + k : first + k + 1] for k in range(4)], axis=1)


def rows_of(line):
    return jnp.concatenate([line[:, 128 * k : 128 * k + 128] for k in range(4)], axis=0)


def kernel(
    q_in, labels, p_in, stat_out, gx, gsc, pg_out,
    protos, qall, raw, expo, grad, pn_line, own_x, stat, term, row_line,
    lab_col, top_col, tot_col, lbl_col,
    xs, xr, xsc, xrc, zs, zr, acc, coltot, pn_own, gbuf,
    in_sem, q_ssem, q_rsem, st_ssem, st_rsem, pb_ssem, pb_rsem,
    x_ssem, x_rsem, xc_ssem, xc_rsem, z_ssem, z_rsem, gz_ssem, gz_rsem,
    gx_ssem, gx_rsem, gc_ssem, gc_rsem,
):
    ci, pi = lax.axis_index("cls"), lax.axis_index("pb")
    z, x, y, core = ci // NX, lax.rem(ci, NX), pi // 2, lax.rem(pi, 2)
    queries, width = q_in.shape
    classes = p_in.shape[0]
    own_rows = pg_out.shape[0]
    factor = 1.0 / math.sqrt(width)
    block = queries // NX
    part = block // PARTS
    first_class = ci * classes

    def at_x(d):
        return lax.rem(x + d, NX)

    def at_z(d):
        return lax.rem(z + d, NZ)

    def dev_x(d):
        return (z * NX + at_x(d), pi)

    def dev_z(d):
        return (at_z(d) * NX + x, pi)

    def dev_pb(dy, other):
        return (ci, lax.rem(y + dy, NY) * 2 + lax.rem(core + other, 2))

    def pb_of(slot):
        dy, other = SLOTS[slot]
        return lax.rem(y + dy, NY) * 2 + lax.rem(core + other, 2)

    def send(src, dst, ssem, rsem, dev):
        copy = pltpu.make_async_remote_copy(
            src_ref=src, dst_ref=dst, send_sem=ssem, recv_sem=rsem, device_id=dev, device_id_type=MESH
        )
        copy.start()
        return copy

    def arrived(ref, ssem, rsem):
        pltpu.make_async_remote_copy(
            src_ref=ref, dst_ref=ref, send_sem=ssem, recv_sem=rsem, device_id=(ci, pi), device_id_type=MESH
        ).wait_recv()

    sent = []

    sub = 256
    chunk = 1024
    subs = chunk // sub
    chunks = classes // chunk
    q_load = pltpu.make_async_copy(q_in, qall.at[0], in_sem.at[classes // sub])
    q_load.start()

    def p_load(k):
        at = pl.ds(pl.multiple_of(k * sub, sub), sub)
        return pltpu.make_async_copy(p_in.at[at], protos.at[at], in_sem.at[k])

    for k in range(classes // sub):
        p_load(k).start()

    barrier = pltpu.get_barrier_semaphore()
    group = NX * NZ

    @pl.loop(1, group)
    def _(d):
        dev = (lax.rem(ci + d, group), pi)
        pl.semaphore_signal(barrier, inc=1, device_id=dev, device_id_type=MESH)

    for s in range(1, 2 * NY):
        pl.semaphore_signal(barrier, inc=1, device_id=dev_pb(*SLOTS[s]), device_id_type=MESH)

    q_load.wait()
    my_label = lanes_of(labels[pi], 0)
    lab_col[...] = jnp.broadcast_to(my_label - first_class, (128, queries)).T

    for k in range(queries // 128):
        q32 = qall[0, pl.ds(k * 128, 128), :].astype(jnp.float32)
        q32 = q32 * q32
        part_sum = sum(q32[:, 128 * i : 128 * i + 128] for i in range(width // 128))
        row_line[1:2, 128 * k : 128 * k + 128] = factor * jnp.sum(part_sum.T, axis=0, keepdims=True)

    half = queries // 2
    halves = (pl.ds(0, half), pl.ds(half, half))
    slot_at = {s: n for n, s in enumerate(SLOTS)}
    up, down = dev_pb(1, 0), dev_pb(NY - 1, 0)
    sibling = dev_pb(0, 1)

    def q_send(src_slot, dst_slot, rows, n, dev):
        sent.append(
            send(qall.at[src_slot, rows], qall.at[dst_slot, rows], q_ssem.at[n], q_rsem.at[n], dev)
        )

    def q_wait(slot, rows, n):
        arrived(qall.at[slot, rows], q_ssem.at[n], q_rsem.at[n])

    def start_queries():
        pl.semaphore_wait(barrier, group - 1 + 2 * NY - 1)
        q_send(0, slot_at[3, 0], halves[0], 0, up)
        q_send(0, slot_at[1, 0], halves[1], 2, down)
        q_send(0, slot_at[0, 1], halves[0], 6, sibling)
        q_send(0, slot_at[0, 1], halves[1], 7, sibling)
        q_send(0, slot_at[3, 0], halves[1], 1, up)
        q_send(0, slot_at[1, 0], halves[0], 3, down)


    lane = lax.broadcasted_iota(jnp.int32, (16, 128), 1)
    tiles = chunk // 128
    row_step = queries // subs

    def logits_of(k, n):
        p_load(k * subs + n).wait()
        base = pl.multiple_of(k * chunk + n * sub, sub)
        for i in range(sub // 128):
            p32 = protos[pl.ds(base + i * 128, 128), :].astype(jnp.float32)
            p32 = p32 * p32
            part_sum = sum(p32[:, 128 * m : 128 * m + 128] for m in range(width // 128))
            pn_line[0:1, pl.ds(base + i * 128, 128)] = factor * jnp.sum(part_sum.T, axis=0, keepdims=True)
        at = pl.ds(base, sub)
        inner = dot(qall[0], protos[at, :], NT)
        raw[k % 2][:, pl.ds(pl.multiple_of(n * sub, sub), sub)] = inner * (2.0 * factor) - pn_line[0:1, at]

    def exp_of(k, n):
        for r in range(row_step // 16):
            rows = pl.ds(pl.multiple_of(n * row_step + r * 16, 16), 16)
            line = [raw[k % 2][rows, 128 * t : 128 * t + 128] for t in range(tiles)]
            top = line[0]
            for t in line[1:]:
                top = jnp.maximum(top, t)
            label = lab_col[rows, :] - lane
            total = jnp.zeros((16, 128), jnp.float32)
            mine = lbl_col[rows, :] if k else jnp.zeros((16, 128), jnp.float32)
            for t, value in enumerate(line):
                mine = mine + jnp.where(label == k * chunk + 128 * t, value, 0.0)
                e = jnp.exp(value - top)
                total = total + e
                expo[k][rows, 128 * t : 128 * t + 128] = e
            top_col[k, rows, :] = top
            tot_col[k, rows, :] = total
            lbl_col[rows, :] = mine

    for k in range(chunks + 1):

        @pl.loop(0, subs)
        def _(n):
            if k < chunks:
                logits_of(k, n)
            if k:
                exp_of(k - 1, n)

        if k == 0:
            start_queries()

    q_line = row_line[1:2, :]
    top_all = top_col[0]
    for k in range(1, chunks):
        top_all = jnp.maximum(top_all, top_col[k])
    tot_all = sum(tot_col[k] * jnp.exp(top_col[k] - top_all) for k in range(chunks))
    top_all = top_all.T
    m_line = jnp.max(top_all, axis=0, keepdims=True)
    t_line = jnp.sum(tot_all.T * jnp.exp(top_all - m_line), axis=0, keepdims=True)
    l_line = jnp.sum(lbl_col[...].T, axis=0, keepdims=True)
    has = jnp.logical_and(my_label >= first_class, my_label < first_class + classes)
    l_line = jnp.where(has, l_line - q_line, 0.0)
    stat[ci] = jnp.concatenate([rows_of(m_line - q_line + jnp.log(t_line)), rows_of(l_line)], axis=0)

    @pl.loop(1, group)
    def _(d):
        dev = (lax.rem(ci + d, group), pi)
        send(stat.at[ci], stat.at[ci], st_ssem, st_rsem, dev)

    arrived(stat.at[pl.ds(0, group - 1)], st_ssem, st_rsem)
    top = stat[0]
    for k in range(1, group):
        top = jnp.maximum(top, stat[k])
    upper = lax.broadcasted_iota(jnp.int32, (8, 128), 0) < 4
    total = sum(jnp.exp(stat[k] - top) for k in range(group))
    stats = jnp.where(upper, top + jnp.log(total), sum(stat[k] for k in range(group)))
    stat_out[...] = stats
    log_total = lanes_of(stats, 0)

    mine_line = log_total + q_line
    term[0] = jnp.concatenate([rows_of(mine_line), rows_of(mine_line)], axis=0)
    shift = jnp.broadcast_to(mine_line, (128, queries)).T
    for k in range(chunks):
        top_col[k] = jnp.exp(top_col[k] - shift)

    def send_terms():
        for s in range(1, 2 * NY):
            dy, other = SLOTS[s]
            dst = slot_at[(NY - dy) % NY, other]
            sent.append(send(term.at[0], term.at[dst], pb_ssem.at[s], pb_rsem.at[dst], dev_pb(dy, other)))

    def grad_rows(r):
        rows = pl.ds(pl.multiple_of(r * 16, 16), 16)
        label = lab_col[rows, :] - lane
        for k in range(chunks):
            w = top_col[k, rows, :]
            for t in range(tiles):
                at = k * chunk + 128 * t
                g = expo[k][rows, 128 * t : 128 * t + 128] * w
                g = g - jnp.where(label == at, 1.0, 0.0)
                grad[rows, at : at + 128] = g.astype(jnp.bfloat16)

    def x_send(d, h):
        rows = pl.ds(h * part, part)
        at = d - 1
        sent.append(send(xs.at[at, rows], xr.at[at, rows], x_ssem.at[at, h], x_rsem.at[at, h], dev_x(d)))

    for d in (2, 1, 3, 0):
        at = pl.multiple_of(at_x(d) * block, block)

        @pl.loop(0, block // 16)
        def _(r):
            grad_rows(at_x(d) * (block // 16) + r)

        @pl.loop(0, width // 512)
        def _(n):
            cols = pl.ds(pl.multiple_of(n * 512, 512), 512)
            v = dot(grad[pl.ds(at, block), :], protos[:, cols], NN)
            if d:
                power, lines = coded(v)
                xs[d - 1, :, cols] = lines
                for m in range(4):
                    xsc[d - 1, pl.ds(n * 4 + m, 1), :] = scale_of(power[:, 128 * m : 128 * m + 128])
            else:
                own_x[:, cols] = v

        if d:
            sent.append(send(xsc.at[d - 1], xrc.at[d - 1], xc_ssem.at[d - 1], xc_rsem.at[d - 1], dev_x(d)))
            x_send(d, 0)
        if d == 3:
            for e in (2, 1, 3):
                for h in range(1, PARTS):
                    x_send(e, h)
            send_terms()

    own_at = pl.multiple_of(pi * own_rows, own_rows)
    for i in range(own_rows // 128):
        p32 = protos[pl.ds(own_at + i * 128, 128), :].astype(jnp.float32)
        p32 = p32 * p32
        part_sum = sum(p32[:, 128 * n : 128 * n + 128] for n in range(width // 128))
        total = jnp.sum(part_sum, axis=1, keepdims=True) * factor
        pn_own[pl.ds(i * 128, 128), :] = jnp.broadcast_to(total, (128, 128))

    def proto_block(slot):
        pb = pb_of(slot)
        if slot:
            arrived(term.at[slot], pb_ssem.at[slot], pb_rsem.at[slot])
        shift = lanes_of(term[slot], 0)
        label = lanes_of(labels[pb], 0) - first_class - own_at
        for n in range(queries // 256):
            at = slice(256 * n, 256 * n + 256)
            inner = dot(protos[pl.ds(own_at, own_rows), :], qall[slot, at, :], NT)
            pn = pn_own[...]
            pn = jnp.concatenate([pn, pn], axis=1)
            g = jnp.exp(inner * (2.0 * factor) - pn - shift[:, at])
            index = lax.broadcasted_iota(jnp.int32, (own_rows, 256), 0)
            g = (g - jnp.where(index == label[:, at], 1.0, 0.0)).astype(jnp.bfloat16)
            gbuf[:, at] = g
            g32 = g.astype(jnp.float32)
            col = g32[:, 0:128] + g32[:, 128:256]
            if slot or n:
                coltot[...] += col
            else:
                coltot[...] = col

        @pl.loop(0, width // 256)
        def _(n):
            cols = pl.ds(pl.multiple_of(n * 256, 256), 256)
            moment = dot(gbuf[...], qall[slot, :, cols], NN)
            if slot:
                acc[:, cols] += moment
            else:
                acc[:, cols] = moment

    def x_done(h):
        rows = pl.ds(h * part, part)
        for d in (1, 3, 2):
            if h == 0:
                arrived(xrc.at[d - 1], xc_ssem.at[d - 1], xc_rsem.at[d - 1])
            arrived(xr.at[d - 1, rows], x_ssem.at[d - 1, h], x_rsem.at[d - 1, h])
        for n in range(NZ):
            cols = slice(128 * n, 128 * n + 128)
            v = own_x[rows, cols]
            for d in range(1, NX):
                v = v + xr[d - 1, rows, cols].astype(jnp.float32) * xrc[d - 1, n : n + 1, :]
            own_x[rows, cols] = v
            power, lines = coded(v)
            zs[h, n, 0:part, :] = lines
            zs[h, n, part : part + 16, :] = rows16(power)
        for d in (4, 3, 5, 2, 6, 1, 7):
            sent.append(send(zs.at[h, at_z(d)], zr.at[h, d], z_ssem.at[h, d], z_rsem.at[h, d], dev_z(d)))

    def z_done(h):
        for d in (1, 7, 2, 6, 3, 5, 4):
            arrived(zr.at[h, d], z_ssem.at[h, d], z_rsem.at[h, d])
        v = own_x[pl.ds(h * part, part), pl.ds(pl.multiple_of(z * 128, 128), 128)]
        for d in range(1, NZ):
            s = scale_of(zr[h, d, part : part + 16, :])[0:1]
            v = v + zr[h, d, 0:part, :].astype(jnp.float32) * s
        power, lines = coded(v * (2.0 * factor))
        gx[h, x, z, 0:part, :] = lines
        gx[h, x, z, part : part + 16, :] = rows16(power)
        for d in (4, 3, 5, 2, 6, 1, 7):
            sent.append(send(gx.at[h, x, z], gx.at[h, x, z], gz_ssem.at[h, d], gz_rsem.at[h, z], dev_z(d)))

    def gz_done(h):
        for d in (1, 7, 2, 6, 3, 5, 4):
            arrived(gx.at[h, x, at_z(d)], gz_ssem.at[h, d], gz_rsem.at[h, at_z(d)])
        gsc[h, x] = jnp.concatenate(
            [scale_of(gx[h, x, n, part : part + 16, :])[0:1] for n in range(NZ)], axis=0
        )
        for d in (2, 1, 3):
            sent.append(send(gsc.at[h, x], gsc.at[h, x], gc_ssem.at[h, d], gc_rsem.at[h, x], dev_x(d)))
            lines = gx.at[h, x, pl.ds(0, NZ), pl.ds(0, part)]
            sent.append(send(lines, lines, gx_ssem.at[h, d], gx_rsem.at[h, x], dev_x(d)))

    def gx_done(h):
        for d in (1, 3, 2):
            k = at_x(d)
            arrived(gsc.at[h, k], gc_ssem.at[h, d], gc_rsem.at[h, k])
            arrived(gx.at[h, k, pl.ds(0, NZ), pl.ds(0, part)], gx_ssem.at[h, d], gx_rsem.at[h, k])

    def to_other_core(slot, first):
        dy = SLOTS[slot][0]
        for k in range(2):
            q_send(slot, slot_at[dy, 1], halves[k], first + k, sibling)

    def relay():
        q_wait(slot_at[3, 0], halves[0], 0)
        q_send(slot_at[3, 0], slot_at[2, 0], halves[0], 4, up)
        q_wait(slot_at[1, 0], halves[1], 2)
        q_send(slot_at[1, 0], slot_at[2, 0], halves[1], 5, down)

    proto_block(0)
    x_done(0)
    relay()
    q_wait(slot_at[0, 1], halves[0], 6)
    q_wait(slot_at[0, 1], halves[1], 7)
    proto_block(1)
    x_done(1)
    q_wait(slot_at[3, 0], halves[1], 1)
    to_other_core(2, 8)
    proto_block(2)
    z_done(0)
    q_wait(slot_at[1, 0], halves[0], 3)
    to_other_core(3, 10)
    proto_block(3)
    z_done(1)
    for k in range(2):
        q_wait(slot_at[3, 1], halves[k], 8 + k)
    proto_block(4)
    gz_done(0)
    for k in range(2):
        q_wait(slot_at[1, 1], halves[k], 10 + k)
    proto_block(5)
    gz_done(1)
    q_wait(slot_at[2, 0], halves[0], 4)
    q_wait(slot_at[2, 0], halves[1], 5)
    to_other_core(6, 12)
    proto_block(6)
    for k in range(2):
        q_wait(slot_at[2, 1], halves[k], 12 + k)
    proto_block(7)

    @pl.loop(0, own_rows // 128)
    def _(i):
        rows = pl.ds(pl.multiple_of(i * 128, 128), 128)
        own = protos[pl.ds(pl.multiple_of(own_at + i * 128, 128), 128), :].astype(jnp.float32)
        total = jnp.sum(coltot[rows, :], axis=1, keepdims=True)
        pg_out[rows, :] = (2.0 * factor) * (acc[rows, :] - total * own)

    for h in range(PARTS):
        gx_done(h)
    for copy in sent:
        copy.wait_send()
    pltpu.make_async_remote_copy(
        src_ref=stat.at[pl.ds(0, group - 1)], dst_ref=stat.at[pl.ds(0, group - 1)],
        send_sem=st_ssem, recv_sem=st_rsem, device_id=(ci, pi), device_id_type=MESH,
    ).wait_send()


def finish(stats, gx, gsc, pg, loss_out, qg_out, pg_out, loss, lines, sem):
    part = gx.shape[3] - 16
    block = PARTS * part
    copies = [pltpu.make_async_copy(pg, pg_out, sem.at[NX])]
    loss[...] = stats[0:4] - stats[4:8]
    copies.append(pltpu.make_async_copy(loss, loss_out, sem.at[NX + 1]))
    for copy in copies:
        copy.start()
    for k in range(NX):
        for h in range(PARTS):
            at = k * block + h * part
            for n in range(NZ):
                value = gx[h, k, n, 0:part, :].astype(jnp.float32) * gsc[h, k, n : n + 1, :]
                lines[at : at + part, 128 * n : 128 * n + 128] = value
        rows = pl.ds(k * block, block)
        copies.append(pltpu.make_async_copy(lines.at[rows], qg_out.at[rows], sem.at[k]))
        copies[-1].start()
    for copy in copies:
        copy.wait()


def local(queries, labels, prototypes):
    rows, width = queries.shape
    classes = prototypes.shape[0]
    own_rows = classes // (2 * NY)
    block = rows // NX
    part = block // PARTS
    vmem = pltpu.VMEM
    dma = pltpu.SemaphoreType.DMA
    f32, bf16, i16 = jnp.float32, jnp.bfloat16, jnp.int16
    sent_block = (PARTS, NX, NZ, part + 16, 128)
    scratch = [
        vmem((classes, width), bf16),
        vmem((2 * NY, rows, width), bf16),
        [vmem((rows, 1024), f32)] * 2,
        [vmem((rows, 1024), f32)] * (classes // 1024),
        vmem((rows, classes), bf16),
        vmem((8, classes), f32),
        vmem((block, width), f32),
        vmem((NX * NZ, 8, 128), f32),
        vmem((2 * NY, 8, 128), f32),
        vmem((8, rows), f32),
        vmem((rows, 128), jnp.int32),
        vmem((classes // 1024, rows, 128), f32),
        vmem((classes // 1024, rows, 128), f32),
        vmem((rows, 128), f32),
        vmem((NX - 1, block, width), i16),
        vmem((NX - 1, block, width), i16),
        vmem((NX - 1, 8, 128), f32),
        vmem((NX - 1, 8, 128), f32),
        vmem((PARTS, NZ, part + 16, 128), i16),
        vmem((PARTS, NZ, part + 16, 128), i16),
        vmem((own_rows, width), f32),
        vmem((own_rows, 128), f32),
        vmem((own_rows, 128), f32),
        vmem((own_rows, rows), bf16),
        dma((classes // 256 + 1,)),
        dma((14,)), dma((14,)),
        dma(()), dma(()),
        dma((8,)), dma((8,)),
        dma((NX - 1, PARTS)), dma((NX - 1, PARTS)),
        dma((NX - 1,)), dma((NX - 1,)),
        dma((PARTS, NZ)), dma((PARTS, NZ)),
        dma((PARTS, NZ)), dma((PARTS, NZ)),
        dma((PARTS, NX)), dma((PARTS, NX)),
        dma((PARTS, NX)), dma((PARTS, NX)),
    ]
    here = pl.BlockSpec(memory_space=pltpu.VMEM)
    anywhere = pl.BlockSpec(memory_space=pl.ANY)
    stats, gx, gsc, pg = pl.pallas_call(
        kernel,
        out_shape=(
            jax.ShapeDtypeStruct((8, 128), f32),
            jax.ShapeDtypeStruct(sent_block, i16),
            jax.ShapeDtypeStruct((PARTS, NX, NZ, 128), f32),
            jax.ShapeDtypeStruct((own_rows, width), f32),
        ),
        in_specs=[anywhere, here, anywhere],
        out_specs=[here] * 4,
        scratch_shapes=scratch,
        compiler_params=pltpu.CompilerParams(
            collective_id=0, has_side_effects=True, vmem_limit_bytes=48 * 2**20
        ),
    )(queries, labels.reshape(2 * NY, 4, rows // 4), prototypes)
    loss, query_grad, proto_grad = pl.pallas_call(
        finish,
        out_shape=(
            jax.ShapeDtypeStruct((4, rows // 4), f32),
            jax.ShapeDtypeStruct((rows, width), f32),
            jax.ShapeDtypeStruct((own_rows, width), f32),
        ),
        in_specs=[here] * 4,
        out_specs=[anywhere] * 3,
        scratch_shapes=[vmem((4, rows // 4), f32), vmem((rows, width), f32), dma((NX + 2,))],
        compiler_params=pltpu.CompilerParams(vmem_limit_bytes=8 * 2**20),
    )(stats, gx, gsc, pg)
    return loss.reshape(rows), query_grad, proto_grad


def solution(mesh):
    placed = (P("pb", None), P(), P("cls", None))
    return jax.shard_map(
        local,
        mesh=mesh,
        in_specs=placed,
        out_specs=(P("pb"), P("pb", None), P(("cls", "pb"), None)),
        check_vma=False,
    )
```

```python
import math

import jax
import jax.numpy as jnp
from jax import lax
from jax.experimental import pallas as pl
from jax.experimental.pallas import tpu as pltpu
from jax.sharding import PartitionSpec as P

MESH = pl.DeviceIdType.MESH
NX, NZ, NY = 4, 8, 4
PARTS = 2
TOP = 32000.0

NT = (((1,), (1,)), ((), ()))
NN = (((1,), (0,)), ((), ()))
SLOTS = ((0, 0), (0, 1), (3, 0), (1, 0), (3, 1), (1, 1), (2, 0), (2, 1))


def dot(a, b, dims):
    return lax.dot_general(a, b, dims, preferred_element_type=jnp.float32)


def coded(value):
    top = jnp.max(jnp.abs(value), axis=0, keepdims=True)
    power = jnp.ceil(jnp.log2(jnp.maximum(top, 1e-30)) + 1e-4)
    lines = jnp.round(value * (jnp.exp2(-power) * TOP))
    lines = jnp.clip(lines, -32767.0, 32767.0)
    return power, lines.astype(jnp.int32).astype(jnp.int16)


def rows16(power):
    return jnp.broadcast_to(power, (16, power.shape[1])).astype(jnp.int32).astype(jnp.int16)


def scale_of(power):
    return jnp.exp2(power.astype(jnp.float32)) * (1.0 / TOP)


def lanes_of(tile, first):
    return jnp.concatenate([tile[first + k : first + k + 1] for k in range(4)], axis=1)


def rows_of(line):
    return jnp.concatenate([line[:, 128 * k : 128 * k + 128] for k in range(4)], axis=0)


def kernel(
    q_in, labels_in, p_in, stat_out, gx, gsc, pg_out,
    labels, protos, qall, raw, expo, grad, pn_line, own_x, stat, term, row_line,
    lab_col, top_col, tot_col, lbl_col,
    xs, xr, xsc, xrc, zs, zr, acc, coltot, pn_own, gbuf, early,
    in_sem, q_ssem, q_rsem, st_ssem, st_rsem, pb_ssem, pb_rsem,
    x_ssem, x_rsem, xc_ssem, xc_rsem, z_ssem, z_rsem, gz_ssem, gz_rsem,
    gx_ssem, gx_rsem, gc_ssem, gc_rsem,
):
    ci, pi = lax.axis_index("cls"), lax.axis_index("pb")
    z, x, y, core = ci // NX, lax.rem(ci, NX), pi // 2, lax.rem(pi, 2)
    queries, width = q_in.shape
    classes = p_in.shape[0]
    own_rows = pg_out.shape[0]
    factor = 1.0 / math.sqrt(width)
    block = queries // NX
    part = block // PARTS
    first_class = ci * classes

    def at_x(d):
        return lax.rem(x + d, NX)

    def at_z(d):
        return lax.rem(z + d, NZ)

    def dev_x(d):
        return (z * NX + at_x(d), pi)

    def dev_z(d):
        return (at_z(d) * NX + x, pi)

    def dev_pb(dy, other):
        return (ci, lax.rem(y + dy, NY) * 2 + lax.rem(core + other, 2))

    def pb_of(slot):
        dy, other = SLOTS[slot]
        return lax.rem(y + dy, NY) * 2 + lax.rem(core + other, 2)

    def send(src, dst, ssem, rsem, dev):
        copy = pltpu.make_async_remote_copy(
            src_ref=src, dst_ref=dst, send_sem=ssem, recv_sem=rsem, device_id=dev, device_id_type=MESH
        )
        copy.start()
        return copy

    def arrived(ref, ssem, rsem):
        pltpu.make_async_remote_copy(
            src_ref=ref, dst_ref=ref, send_sem=ssem, recv_sem=rsem, device_id=(ci, pi), device_id_type=MESH
        ).wait_recv()

    sent = []

    sub = 256
    chunk = 1024
    subs = chunk // sub
    chunks = classes // chunk
    q_load = pltpu.make_async_copy(q_in, qall.at[0], in_sem.at[classes // sub])
    q_load.start()
    label_load = pltpu.make_async_copy(labels_in, labels, in_sem.at[classes // sub + 1])
    label_load.start()

    def p_load(k):
        at = pl.ds(pl.multiple_of(k * sub, sub), sub)
        return pltpu.make_async_copy(p_in.at[at], protos.at[at], in_sem.at[k])

    for k in range(classes // sub):
        p_load(k).start()

    barrier = pltpu.get_barrier_semaphore()
    group = NX * NZ

    @pl.loop(1, group)
    def _(d):
        dev = (lax.rem(ci + d, group), pi)
        pl.semaphore_signal(barrier, inc=1, device_id=dev, device_id_type=MESH)

    for s in range(1, 2 * NY):
        pl.semaphore_signal(barrier, inc=1, device_id=dev_pb(*SLOTS[s]), device_id_type=MESH)

    label_load.wait()
    my_label = lanes_of(labels[pi], 0)
    lab_col[...] = jnp.broadcast_to(my_label - first_class, (128, queries)).T

    q_load.wait()
    for k in range(queries // 128):
        q32 = qall[0, pl.ds(k * 128, 128), :].astype(jnp.float32)
        q32 = q32 * q32
        part_sum = sum(q32[:, 128 * i : 128 * i + 128] for i in range(width // 128))
        row_line[1:2, 128 * k : 128 * k + 128] = factor * jnp.sum(part_sum.T, axis=0, keepdims=True)

    half = queries // 2
    halves = (pl.ds(0, half), pl.ds(half, half))
    slot_at = {s: n for n, s in enumerate(SLOTS)}
    up, down = dev_pb(1, 0), dev_pb(NY - 1, 0)
    sibling = dev_pb(0, 1)

    def q_send(src_slot, dst_slot, rows, n, dev):
        sent.append(
            send(qall.at[src_slot, rows], qall.at[dst_slot, rows], q_ssem.at[n], q_rsem.at[n], dev)
        )

    def q_wait(slot, rows, n):
        arrived(qall.at[slot, rows], q_ssem.at[n], q_rsem.at[n])

    def start_queries():
        q_send(0, slot_at[3, 0], halves[0], 0, up)
        q_send(0, slot_at[1, 0], halves[1], 2, down)
        q_send(0, slot_at[0, 1], halves[0], 6, sibling)
        q_send(0, slot_at[0, 1], halves[1], 7, sibling)
        q_send(0, slot_at[3, 0], halves[1], 1, up)
        q_send(0, slot_at[1, 0], halves[0], 3, down)


    lane = lax.broadcasted_iota(jnp.int32, (16, 128), 1)
    tiles = chunk // 128
    row_step = queries // subs

    def logits_of(k, n):
        p_load(k * subs + n).wait()
        base = pl.multiple_of(k * chunk + n * sub, sub)
        for i in range(sub // 128):
            p32 = protos[pl.ds(base + i * 128, 128), :].astype(jnp.float32)
            p32 = p32 * p32
            part_sum = sum(p32[:, 128 * m : 128 * m + 128] for m in range(width // 128))
            pn_line[0:1, pl.ds(base + i * 128, 128)] = factor * jnp.sum(part_sum.T, axis=0, keepdims=True)
        at = pl.ds(base, sub)
        inner = dot(qall[0], protos[at, :], NT)
        raw[k % 2][:, pl.ds(pl.multiple_of(n * sub, sub), sub)] = inner * (2.0 * factor) - pn_line[0:1, at]

    def exp_of(k, n):
        for r in range(row_step // 16):
            rows = pl.ds(pl.multiple_of(n * row_step + r * 16, 16), 16)
            line = [raw[k % 2][rows, 128 * t : 128 * t + 128] for t in range(tiles)]
            top = line[0]
            for t in line[1:]:
                top = jnp.maximum(top, t)
            label = lab_col[rows, :] - lane
            total = jnp.zeros((16, 128), jnp.float32)
            mine = lbl_col[rows, :] if k else jnp.zeros((16, 128), jnp.float32)
            for t, value in enumerate(line):
                mine = mine + jnp.where(label == k * chunk + 128 * t, value, 0.0)
                e = jnp.exp(value - top)
                total = total + e
                expo[k][rows, 128 * t : 128 * t + 128] = e
            top_col[k, rows, :] = top
            tot_col[k, rows, :] = total
            lbl_col[rows, :] = mine

    for k in range(chunks + 1):

        @pl.loop(0, subs)
        def _(n):
            if k < chunks:
                logits_of(k, n)
            if k:
                exp_of(k - 1, n)

        if k == 1:
            pl.semaphore_wait(barrier, group - 1 + 2 * NY - 1)
            start_queries()

    q_line = row_line[1:2, :]
    top_all = top_col[0]
    for k in range(1, chunks):
        top_all = jnp.maximum(top_all, top_col[k])
    tot_all = sum(tot_col[k] * jnp.exp(top_col[k] - top_all) for k in range(chunks))
    top_all = top_all.T
    m_line = jnp.max(top_all, axis=0, keepdims=True)
    t_line = jnp.sum(tot_all.T * jnp.exp(top_all - m_line), axis=0, keepdims=True)
    l_line = jnp.sum(lbl_col[...].T, axis=0, keepdims=True)
    has = jnp.logical_and(my_label >= first_class, my_label < first_class + classes)
    l_line = jnp.where(has, l_line - q_line, 0.0)
    stat[ci] = jnp.concatenate([rows_of(m_line - q_line + jnp.log(t_line)), rows_of(l_line)], axis=0)

    @pl.loop(1, group)
    def _(d):
        dev = (lax.rem(ci + d, group), pi)
        send(stat.at[ci], stat.at[ci], st_ssem, st_rsem, dev)

    own_at = pl.multiple_of(pi * own_rows, own_rows)
    for i in range(own_rows // 128):
        p32 = protos[pl.ds(own_at + i * 128, 128), :].astype(jnp.float32)
        p32 = p32 * p32
        part_sum = sum(p32[:, 128 * n : 128 * n + 128] for n in range(width // 128))
        total = jnp.sum(part_sum, axis=1, keepdims=True) * factor
        pn_own[pl.ds(i * 128, 128), :] = jnp.broadcast_to(total, (128, 128))

    for slot in range(2):
        if slot:
            for k in range(2):
                q_wait(slot_at[0, 1], halves[k], 6 + k)

        @pl.loop(0, queries // 256)
        def _(n):
            at = pl.ds(pl.multiple_of(n * 256, 256), 256)
            early[slot, :, at] = dot(protos[pl.ds(own_at, own_rows), :], qall[slot, at, :], NT)

    arrived(stat.at[pl.ds(0, group - 1)], st_ssem, st_rsem)
    top = stat[0]
    for k in range(1, group):
        top = jnp.maximum(top, stat[k])
    upper = lax.broadcasted_iota(jnp.int32, (8, 128), 0) < 4
    total = sum(jnp.exp(stat[k] - top) for k in range(group))
    stats = jnp.where(upper, top + jnp.log(total), sum(stat[k] for k in range(group)))
    stat_out[...] = stats
    log_total = lanes_of(stats, 0)

    mine_line = log_total + q_line
    term[0] = jnp.concatenate([rows_of(mine_line), rows_of(mine_line)], axis=0)
    shift = jnp.broadcast_to(mine_line, (128, queries)).T
    for k in range(chunks):
        top_col[k] = jnp.exp(top_col[k] - shift)

    def send_terms():
        for s in range(1, 2 * NY):
            dy, other = SLOTS[s]
            dst = slot_at[(NY - dy) % NY, other]
            sent.append(send(term.at[0], term.at[dst], pb_ssem.at[s], pb_rsem.at[dst], dev_pb(dy, other)))

    def grad_rows(r):
        rows = pl.ds(pl.multiple_of(r * 16, 16), 16)
        label = lab_col[rows, :] - lane
        for k in range(chunks):
            w = top_col[k, rows, :]
            for t in range(tiles):
                at = k * chunk + 128 * t
                g = expo[k][rows, 128 * t : 128 * t + 128] * w
                g = g - jnp.where(label == at, 1.0, 0.0)
                grad[rows, at : at + 128] = g.astype(jnp.bfloat16)

    def x_send(d, h):
        rows = pl.ds(h * part, part)
        at = d - 1
        return send(xs.at[at, rows], xr.at[at, rows], x_ssem.at[at, h], x_rsem.at[at, h], dev_x(d))

    moving = {}
    order = (2, 1, 3, 0)
    steps = block // 16
    turns = width // 512

    @pl.loop(0, steps)
    def _(r):
        grad_rows(at_x(order[0]) * steps + r)

    for i, d in enumerate(order):
        at = pl.multiple_of(at_x(d) * block, block)

        @pl.loop(0, turns)
        def _(n):
            cols = pl.ds(pl.multiple_of(n * 512, 512), 512)
            if i + 1 < len(order):
                for r in range(steps // turns):
                    grad_rows(at_x(order[i + 1]) * steps + n * (steps // turns) + r)
            v = dot(grad[pl.ds(at, block), :], protos[:, cols], NN)
            if d:
                power, lines = coded(v)
                xs[d - 1, :, cols] = lines
                for m in range(4):
                    xsc[d - 1, pl.ds(n * 4 + m, 1), :] = scale_of(power[:, 128 * m : 128 * m + 128])
            else:
                own_x[:, cols] = v

        if d:
            sent.append(send(xsc.at[d - 1], xrc.at[d - 1], xc_ssem.at[d - 1], xc_rsem.at[d - 1], dev_x(d)))
            moving[d] = x_send(d, 0)
        if d == 3:
            send_terms()
            for h in range(1, PARTS):
                for e in (2, 1, 3):
                    sent.append(moving[e])
                    moving[e] = x_send(e, h)
    sent.extend(moving.values())

    def proto_block(slot):
        pb = pb_of(slot)
        if slot:
            arrived(term.at[slot], pb_ssem.at[slot], pb_rsem.at[slot])
        shift = lanes_of(term[slot], 0)
        label = lanes_of(labels[pb], 0) - first_class - own_at
        for n in range(queries // 256):
            at = slice(256 * n, 256 * n + 256)
            if slot < 2:
                inner = early[slot, :, at]
            else:
                inner = dot(protos[pl.ds(own_at, own_rows), :], qall[slot, at, :], NT)
            pn = pn_own[...]
            pn = jnp.concatenate([pn, pn], axis=1)
            g = jnp.exp(inner * (2.0 * factor) - pn - shift[:, at])
            index = lax.broadcasted_iota(jnp.int32, (own_rows, 256), 0)
            g = (g - jnp.where(index == label[:, at], 1.0, 0.0)).astype(jnp.bfloat16)
            gbuf[:, at] = g
            g32 = g.astype(jnp.float32)
            col = g32[:, 0:128] + g32[:, 128:256]
            if slot or n:
                coltot[...] += col
            else:
                coltot[...] = col

        @pl.loop(0, width // 256)
        def _(n):
            cols = pl.ds(pl.multiple_of(n * 256, 256), 256)
            moment = dot(gbuf[...], qall[slot, :, cols], NN)
            if slot:
                acc[:, cols] += moment
            else:
                acc[:, cols] = moment

    def x_done(h):
        rows = pl.ds(h * part, part)
        for d in (1, 3, 2):
            if h == 0:
                arrived(xrc.at[d - 1], xc_ssem.at[d - 1], xc_rsem.at[d - 1])
            arrived(xr.at[d - 1, rows], x_ssem.at[d - 1, h], x_rsem.at[d - 1, h])
        for n in range(NZ):
            cols = slice(128 * n, 128 * n + 128)
            v = own_x[rows, cols]
            for d in range(1, NX):
                v = v + xr[d - 1, rows, cols].astype(jnp.float32) * xrc[d - 1, n : n + 1, :]
            own_x[rows, cols] = v
            power, lines = coded(v)
            zs[h, n, 0:part, :] = lines
            zs[h, n, part : part + 16, :] = rows16(power)
        for d in (4, 3, 5, 2, 6, 1, 7):
            sent.append(send(zs.at[h, at_z(d)], zr.at[h, d], z_ssem.at[h, d], z_rsem.at[h, d], dev_z(d)))

    def z_done(h):
        for d in (1, 7, 2, 6, 3, 5, 4):
            arrived(zr.at[h, d], z_ssem.at[h, d], z_rsem.at[h, d])
        v = own_x[pl.ds(h * part, part), pl.ds(pl.multiple_of(z * 128, 128), 128)]
        for d in range(1, NZ):
            s = scale_of(zr[h, d, part : part + 16, :])[0:1]
            v = v + zr[h, d, 0:part, :].astype(jnp.float32) * s
        power, lines = coded(v * (2.0 * factor))
        gx[h, x, z, 0:part, :] = lines
        gx[h, x, z, part : part + 16, :] = rows16(power)
        for d in (4, 3, 5, 2, 6, 1, 7):
            sent.append(send(gx.at[h, x, z], gx.at[h, x, z], gz_ssem.at[h, d], gz_rsem.at[h, z], dev_z(d)))

    def gz_done(h):
        for d in (1, 7, 2, 6, 3, 5, 4):
            arrived(gx.at[h, x, at_z(d)], gz_ssem.at[h, d], gz_rsem.at[h, at_z(d)])
        gsc[h, x] = jnp.concatenate(
            [scale_of(gx[h, x, n, part : part + 16, :])[0:1] for n in range(NZ)], axis=0
        )
        for d in (2, 1, 3):
            sent.append(send(gsc.at[h, x], gsc.at[h, x], gc_ssem.at[h, d], gc_rsem.at[h, x], dev_x(d)))
            lines = gx.at[h, x, pl.ds(0, NZ), pl.ds(0, part)]
            sent.append(send(lines, lines, gx_ssem.at[h, d], gx_rsem.at[h, x], dev_x(d)))

    def gx_done(h):
        for d in (1, 3, 2):
            k = at_x(d)
            arrived(gsc.at[h, k], gc_ssem.at[h, d], gc_rsem.at[h, k])
            arrived(gx.at[h, k, pl.ds(0, NZ), pl.ds(0, part)], gx_ssem.at[h, d], gx_rsem.at[h, k])

    def to_other_core(slot, first):
        dy = SLOTS[slot][0]
        for k in range(2):
            q_send(slot, slot_at[dy, 1], halves[k], first + k, sibling)

    def relay():
        q_wait(slot_at[3, 0], halves[0], 0)
        q_send(slot_at[3, 0], slot_at[2, 0], halves[0], 4, up)
        q_wait(slot_at[1, 0], halves[1], 2)
        q_send(slot_at[1, 0], slot_at[2, 0], halves[1], 5, down)

    proto_block(0)
    x_done(0)
    relay()
    proto_block(1)
    x_done(1)
    q_wait(slot_at[3, 0], halves[1], 1)
    to_other_core(2, 8)
    q_wait(slot_at[1, 0], halves[0], 3)
    to_other_core(3, 10)
    z_done(0)
    proto_block(2)
    z_done(1)
    proto_block(3)
    gz_done(0)
    q_wait(4, halves[0], 8)
    q_wait(4, halves[1], 9)
    proto_block(4)
    gz_done(1)
    q_wait(5, halves[0], 10)
    q_wait(5, halves[1], 11)
    proto_block(5)
    q_wait(slot_at[2, 0], halves[0], 4)
    q_wait(slot_at[2, 0], halves[1], 5)
    to_other_core(6, 12)
    proto_block(6)
    q_wait(7, halves[0], 12)
    q_wait(7, halves[1], 13)
    proto_block(7)

    @pl.loop(0, own_rows // 128)
    def _(i):
        rows = pl.ds(pl.multiple_of(i * 128, 128), 128)
        own = protos[pl.ds(pl.multiple_of(own_at + i * 128, 128), 128), :].astype(jnp.float32)
        total = jnp.sum(coltot[rows, :], axis=1, keepdims=True)
        pg_out[rows, :] = (2.0 * factor) * (acc[rows, :] - total * own)

    late = 2 * PARTS * (NX - 1)
    for copy in sent[:-late]:
        copy.wait_send()
    for h in range(PARTS):
        gx_done(h)
    for copy in sent[-late:]:
        copy.wait_send()
    pltpu.make_async_remote_copy(
        src_ref=stat.at[pl.ds(0, group - 1)], dst_ref=stat.at[pl.ds(0, group - 1)],
        send_sem=st_ssem, recv_sem=st_rsem, device_id=(ci, pi), device_id_type=MESH,
    ).wait_send()


def finish(stats, gx, gsc, pg, loss_out, qg_out, pg_out, loss, lines, sem):
    part = gx.shape[3] - 16
    block = PARTS * part
    copies = [pltpu.make_async_copy(pg, pg_out, sem.at[NX])]
    loss[...] = stats[0:4] - stats[4:8]
    copies.append(pltpu.make_async_copy(loss, loss_out, sem.at[NX + 1]))
    for copy in copies:
        copy.start()
    for k in range(NX):
        for h in range(PARTS):
            at = k * block + h * part
            for n in range(NZ):
                value = gx[h, k, n, 0:part, :].astype(jnp.float32) * gsc[h, k, n : n + 1, :]
                lines[at : at + part, 128 * n : 128 * n + 128] = value
        rows = pl.ds(k * block, block)
        copies.append(pltpu.make_async_copy(lines.at[rows], qg_out.at[rows], sem.at[k]))
        copies[-1].start()
    for copy in copies:
        copy.wait()


def local(queries, labels, prototypes):
    rows, width = queries.shape
    classes = prototypes.shape[0]
    own_rows = classes // (2 * NY)
    block = rows // NX
    part = block // PARTS
    vmem = pltpu.VMEM
    dma = pltpu.SemaphoreType.DMA
    f32, bf16, i16 = jnp.float32, jnp.bfloat16, jnp.int16
    sent_block = (PARTS, NX, NZ, part + 16, 128)
    scratch = [
        vmem((2 * NY, 4, rows // 4), jnp.int32),
        vmem((classes, width), bf16),
        vmem((2 * NY, rows, width), bf16),
        [vmem((rows, 1024), f32)] * 2,
        [vmem((rows, 1024), f32)] * (classes // 1024),
        vmem((rows, classes), bf16),
        vmem((8, classes), f32),
        vmem((block, width), f32),
        vmem((NX * NZ, 8, 128), f32),
        vmem((2 * NY, 8, 128), f32),
        vmem((8, rows), f32),
        vmem((rows, 128), jnp.int32),
        vmem((classes // 1024, rows, 128), f32),
        vmem((classes // 1024, rows, 128), f32),
        vmem((rows, 128), f32),
        vmem((NX - 1, block, width), i16),
        vmem((NX - 1, block, width), i16),
        vmem((NX - 1, 8, 128), f32),
        vmem((NX - 1, 8, 128), f32),
        vmem((PARTS, NZ, part + 16, 128), i16),
        vmem((PARTS, NZ, part + 16, 128), i16),
        vmem((own_rows, width), f32),
        vmem((own_rows, 128), f32),
        vmem((own_rows, 128), f32),
        vmem((own_rows, rows), bf16),
        vmem((2, own_rows, rows), f32),
        dma((classes // 256 + 2,)),
        dma((14,)), dma((14,)),
        dma(()), dma(()),
        dma((8,)), dma((8,)),
        dma((NX - 1, PARTS)), dma((NX - 1, PARTS)),
        dma((NX - 1,)), dma((NX - 1,)),
        dma((PARTS, NZ)), dma((PARTS, NZ)),
        dma((PARTS, NZ)), dma((PARTS, NZ)),
        dma((PARTS, NX)), dma((PARTS, NX)),
        dma((PARTS, NX)), dma((PARTS, NX)),
    ]
    here = pl.BlockSpec(memory_space=pltpu.VMEM)
    anywhere = pl.BlockSpec(memory_space=pl.ANY)
    stats, gx, gsc, pg = pl.pallas_call(
        kernel,
        out_shape=(
            jax.ShapeDtypeStruct((8, 128), f32),
            jax.ShapeDtypeStruct(sent_block, i16),
            jax.ShapeDtypeStruct((PARTS, NX, NZ, 128), f32),
            jax.ShapeDtypeStruct((own_rows, width), f32),
        ),
        in_specs=[pl.BlockSpec(memory_space=pltpu.HBM)] * 3,
        out_specs=[here] * 4,
        scratch_shapes=scratch,
        compiler_params=pltpu.CompilerParams(
            collective_id=0, has_side_effects=True, vmem_limit_bytes=48 * 2**20
        ),
    )(queries, labels.reshape(2 * NY, 4, rows // 4), prototypes)
    loss, query_grad, proto_grad = pl.pallas_call(
        finish,
        out_shape=(
            jax.ShapeDtypeStruct((4, rows // 4), f32),
            jax.ShapeDtypeStruct((rows, width), f32),
            jax.ShapeDtypeStruct((own_rows, width), f32),
        ),
        in_specs=[here] * 4,
        out_specs=[anywhere] * 3,
        scratch_shapes=[vmem((4, rows // 4), f32), vmem((rows, width), f32), dma((NX + 2,))],
        compiler_params=pltpu.CompilerParams(vmem_limit_bytes=8 * 2**20),
    )(stats, gx, gsc, pg)
    return loss.reshape(rows), query_grad, proto_grad


def solution(mesh):
    placed = (P("pb", None), P(), P("cls", None))
    return jax.shard_map(
        local,
        mesh=mesh,
        in_specs=placed,
        out_specs=(P("pb"), P("pb", None), P(("cls", "pb"), None)),
        check_vma=False,
    )
```

```python
import math

import jax
import jax.numpy as jnp
from jax import lax
from jax.experimental import pallas as pl
from jax.experimental.pallas import tpu as pltpu
from jax.sharding import PartitionSpec as P

MESH = pl.DeviceIdType.MESH
NX, NZ, NY = 4, 8, 4
PARTS = 2
TOP = 32000.0

NT = (((1,), (1,)), ((), ()))
NN = (((1,), (0,)), ((), ()))
SLOTS = ((0, 0), (0, 1), (3, 0), (1, 0), (3, 1), (1, 1), (2, 0), (2, 1))


def dot(a, b, dims):
    return lax.dot_general(a, b, dims, preferred_element_type=jnp.float32)


def coded(value):
    top = jnp.max(jnp.abs(value), axis=0, keepdims=True)
    power = jnp.ceil(jnp.log2(jnp.maximum(top, 1e-30)) + 1e-4)
    lines = jnp.round(value * (jnp.exp2(-power) * TOP))
    lines = jnp.clip(lines, -32767.0, 32767.0)
    return power, lines.astype(jnp.int32).astype(jnp.int16)


def rows16(power):
    return jnp.broadcast_to(power, (16, power.shape[1])).astype(jnp.int32).astype(jnp.int16)


def scale_of(power):
    return jnp.exp2(power.astype(jnp.float32)) * (1.0 / TOP)


def lanes_of(tile, first):
    return jnp.concatenate([tile[first + k : first + k + 1] for k in range(4)], axis=1)


def rows_of(line):
    return jnp.concatenate([line[:, 128 * k : 128 * k + 128] for k in range(4)], axis=0)


def kernel(
    q_in, labels_in, p_in, stat_out, gx, gsc, pg_out,
    labels, protos, qall, raw, expo, grad, pn_line, own_x, stat, term, row_line,
    lab_col, top_col, tot_col, lbl_col,
    xs, xr, xsc, xrc, zs, zr, acc, coltot, pn_own, gbuf, early,
    in_sem, q_ssem, q_rsem, st_ssem, st_rsem, pb_ssem, pb_rsem,
    x_ssem, x_rsem, xc_ssem, xc_rsem, z_ssem, z_rsem, gz_ssem, gz_rsem,
    gx_ssem, gx_rsem, gc_ssem, gc_rsem,
):
    ci, pi = lax.axis_index("cls"), lax.axis_index("pb")
    z, x, y, core = ci // NX, lax.rem(ci, NX), pi // 2, lax.rem(pi, 2)
    queries, width = q_in.shape
    classes = p_in.shape[0]
    own_rows = pg_out.shape[0]
    factor = 1.0 / math.sqrt(width)
    block = queries // NX
    part = block // PARTS
    first_class = ci * classes

    def at_x(d):
        return lax.rem(x + d, NX)

    def at_z(d):
        return lax.rem(z + d, NZ)

    def dev_x(d):
        return (z * NX + at_x(d), pi)

    def dev_z(d):
        return (at_z(d) * NX + x, pi)

    def dev_pb(dy, other):
        return (ci, lax.rem(y + dy, NY) * 2 + lax.rem(core + other, 2))

    def pb_of(slot):
        dy, other = SLOTS[slot]
        return lax.rem(y + dy, NY) * 2 + lax.rem(core + other, 2)

    def send(src, dst, ssem, rsem, dev):
        copy = pltpu.make_async_remote_copy(
            src_ref=src, dst_ref=dst, send_sem=ssem, recv_sem=rsem, device_id=dev, device_id_type=MESH
        )
        copy.start()
        return copy

    def arrived(ref, ssem, rsem):
        pltpu.make_async_remote_copy(
            src_ref=ref, dst_ref=ref, send_sem=ssem, recv_sem=rsem, device_id=(ci, pi), device_id_type=MESH
        ).wait_recv()

    sent = []

    sub = 256
    chunk = 1024
    subs = chunk // sub
    chunks = classes // chunk
    q_load = pltpu.make_async_copy(q_in, qall.at[0], in_sem.at[classes // sub])
    q_load.start()
    label_load = pltpu.make_async_copy(labels_in, labels, in_sem.at[classes // sub + 1])
    label_load.start()

    def p_load(k):
        at = pl.ds(pl.multiple_of(k * sub, sub), sub)
        return pltpu.make_async_copy(p_in.at[at], protos.at[at], in_sem.at[k])

    for k in range(classes // sub):
        p_load(k).start()

    barrier = pltpu.get_barrier_semaphore()
    group = NX * NZ

    @pl.loop(1, group)
    def _(d):
        dev = (lax.rem(ci + d, group), pi)
        pl.semaphore_signal(barrier, inc=1, device_id=dev, device_id_type=MESH)

    for s in range(1, 2 * NY):
        pl.semaphore_signal(barrier, inc=1, device_id=dev_pb(*SLOTS[s]), device_id_type=MESH)

    label_load.wait()
    my_label = lanes_of(labels[pi], 0)
    lab_col[...] = jnp.broadcast_to(my_label - first_class, (128, queries)).T

    q_load.wait()
    for k in range(queries // 128):
        q32 = qall[0, pl.ds(k * 128, 128), :].astype(jnp.float32)
        q32 = q32 * q32
        part_sum = sum(q32[:, 128 * i : 128 * i + 128] for i in range(width // 128))
        row_line[1:2, 128 * k : 128 * k + 128] = factor * jnp.sum(part_sum.T, axis=0, keepdims=True)

    half = queries // 2
    halves = (pl.ds(0, half), pl.ds(half, half))
    slot_at = {s: n for n, s in enumerate(SLOTS)}
    up, down = dev_pb(1, 0), dev_pb(NY - 1, 0)
    sibling = dev_pb(0, 1)

    def q_send(src_slot, dst_slot, rows, n, dev):
        sent.append(
            send(qall.at[src_slot, rows], qall.at[dst_slot, rows], q_ssem.at[n], q_rsem.at[n], dev)
        )

    def q_wait(slot, rows, n):
        arrived(qall.at[slot, rows], q_ssem.at[n], q_rsem.at[n])

    def start_queries():
        q_send(0, slot_at[3, 0], halves[0], 0, up)
        q_send(0, slot_at[1, 0], halves[1], 2, down)
        q_send(0, slot_at[0, 1], halves[0], 6, sibling)
        q_send(0, slot_at[0, 1], halves[1], 7, sibling)
        q_send(0, slot_at[3, 0], halves[1], 1, up)
        q_send(0, slot_at[1, 0], halves[0], 3, down)


    lane = lax.broadcasted_iota(jnp.int32, (16, 128), 1)
    tiles = chunk // 128
    row_step = queries // subs

    def logits_of(k, n):
        p_load(k * subs + n).wait()
        base = pl.multiple_of(k * chunk + n * sub, sub)
        for i in range(sub // 128):
            p32 = protos[pl.ds(base + i * 128, 128), :].astype(jnp.float32)
            p32 = p32 * p32
            part_sum = sum(p32[:, 128 * m : 128 * m + 128] for m in range(width // 128))
            pn_line[0:1, pl.ds(base + i * 128, 128)] = factor * jnp.sum(part_sum.T, axis=0, keepdims=True)
        at = pl.ds(base, sub)
        inner = dot(qall[0], protos[at, :], NT)
        raw[k % 2][:, pl.ds(pl.multiple_of(n * sub, sub), sub)] = inner * (2.0 * factor) - pn_line[0:1, at]

    def exp_of(k, n):
        for r in range(row_step // 16):
            rows = pl.ds(pl.multiple_of(n * row_step + r * 16, 16), 16)
            line = [raw[k % 2][rows, 128 * t : 128 * t + 128] for t in range(tiles)]
            top = line[0]
            for t in line[1:]:
                top = jnp.maximum(top, t)
            label = lab_col[rows, :] - lane
            total = jnp.zeros((16, 128), jnp.float32)
            mine = lbl_col[rows, :] if k else jnp.zeros((16, 128), jnp.float32)
            for t, value in enumerate(line):
                mine = mine + jnp.where(label == k * chunk + 128 * t, value, 0.0)
                e = jnp.exp(value - top)
                total = total + e
                expo[k][rows, 128 * t : 128 * t + 128] = e
            top_col[k, rows, :] = top
            tot_col[k, rows, :] = total
            lbl_col[rows, :] = mine

    for k in range(chunks + 1):

        @pl.loop(0, subs)
        def _(n):
            if k < chunks:
                logits_of(k, n)
            if k:
                exp_of(k - 1, n)

        if k == 1:
            pl.semaphore_wait(barrier, group - 1 + 2 * NY - 1)
            start_queries()

    q_line = row_line[1:2, :]
    top_all = top_col[0]
    for k in range(1, chunks):
        top_all = jnp.maximum(top_all, top_col[k])
    tot_all = sum(tot_col[k] * jnp.exp(top_col[k] - top_all) for k in range(chunks))
    top_all = top_all.T
    m_line = jnp.max(top_all, axis=0, keepdims=True)
    t_line = jnp.sum(tot_all.T * jnp.exp(top_all - m_line), axis=0, keepdims=True)
    l_line = jnp.sum(lbl_col[...].T, axis=0, keepdims=True)
    has = jnp.logical_and(my_label >= first_class, my_label < first_class + classes)
    l_line = jnp.where(has, l_line - q_line, 0.0)
    stat[ci] = jnp.concatenate([rows_of(m_line - q_line + jnp.log(t_line)), rows_of(l_line)], axis=0)

    @pl.loop(1, group)
    def _(d):
        dev = (lax.rem(ci + d, group), pi)
        send(stat.at[ci], stat.at[ci], st_ssem, st_rsem, dev)

    own_at = pl.multiple_of(pi * own_rows, own_rows)
    for i in range(own_rows // 128):
        p32 = protos[pl.ds(own_at + i * 128, 128), :].astype(jnp.float32)
        p32 = p32 * p32
        part_sum = sum(p32[:, 128 * n : 128 * n + 128] for n in range(width // 128))
        total = jnp.sum(part_sum, axis=1, keepdims=True) * factor
        pn_own[pl.ds(i * 128, 128), :] = jnp.broadcast_to(total, (128, 128))

    for slot in range(2):
        if slot:
            for k in range(2):
                q_wait(slot_at[0, 1], halves[k], 6 + k)

        @pl.loop(0, queries // 256)
        def _(n):
            at = pl.ds(pl.multiple_of(n * 256, 256), 256)
            early[slot, :, at] = dot(protos[pl.ds(own_at, own_rows), :], qall[slot, at, :], NT)

    arrived(stat.at[pl.ds(0, group - 1)], st_ssem, st_rsem)
    top = stat[0]
    for k in range(1, group):
        top = jnp.maximum(top, stat[k])
    upper = lax.broadcasted_iota(jnp.int32, (8, 128), 0) < 4
    total = sum(jnp.exp(stat[k] - top) for k in range(group))
    stats = jnp.where(upper, top + jnp.log(total), sum(stat[k] for k in range(group)))
    stat_out[...] = stats
    log_total = lanes_of(stats, 0)

    mine_line = log_total + q_line
    term[0] = jnp.concatenate([rows_of(mine_line), rows_of(mine_line)], axis=0)
    shift = jnp.broadcast_to(mine_line, (128, queries)).T
    for k in range(chunks):
        top_col[k] = jnp.exp(top_col[k] - shift)

    def send_terms():
        for s in range(1, 2 * NY):
            dy, other = SLOTS[s]
            dst = slot_at[(NY - dy) % NY, other]
            sent.append(send(term.at[0], term.at[dst], pb_ssem.at[s], pb_rsem.at[dst], dev_pb(dy, other)))

    def grad_rows(r):
        rows = pl.ds(pl.multiple_of(r * 16, 16), 16)
        label = lab_col[rows, :] - lane
        for k in range(chunks):
            w = top_col[k, rows, :]
            for t in range(tiles):
                at = k * chunk + 128 * t
                g = expo[k][rows, 128 * t : 128 * t + 128] * w
                g = g - jnp.where(label == at, 1.0, 0.0)
                grad[rows, at : at + 128] = g.astype(jnp.bfloat16)

    def x_send(d, h):
        rows = pl.ds(h * part, part)
        at = d - 1
        return send(xs.at[at, rows], xr.at[at, rows], x_ssem.at[at, h], x_rsem.at[at, h], dev_x(d))

    moving = {}
    order = (1, 3, 2, 0)
    steps = block // 16
    turns = width // 512

    @pl.loop(0, steps)
    def _(r):
        grad_rows(at_x(order[0]) * steps + r)

    for i, d in enumerate(order):
        at = pl.multiple_of(at_x(d) * block, block)

        @pl.loop(0, turns)
        def _(n):
            cols = pl.ds(pl.multiple_of(n * 512, 512), 512)
            if i + 1 < len(order):
                for r in range(steps // turns):
                    grad_rows(at_x(order[i + 1]) * steps + n * (steps // turns) + r)
            v = dot(grad[pl.ds(at, block), :], protos[:, cols], NN)
            if d:
                power, lines = coded(v)
                xs[d - 1, :, cols] = lines
                for m in range(4):
                    xsc[d - 1, pl.ds(n * 4 + m, 1), :] = scale_of(power[:, 128 * m : 128 * m + 128])
            else:
                own_x[:, cols] = v

        if d:
            sent.append(send(xsc.at[d - 1], xrc.at[d - 1], xc_ssem.at[d - 1], xc_rsem.at[d - 1], dev_x(d)))
            moving[d] = x_send(d, 0)
        if d == 2:
            send_terms()
            for h in range(1, PARTS):
                for e in (1, 3, 2):
                    sent.append(moving[e])
                    moving[e] = x_send(e, h)
    sent.extend(moving.values())

    def proto_block(slot):
        pb = pb_of(slot)
        if slot:
            arrived(term.at[slot], pb_ssem.at[slot], pb_rsem.at[slot])
        shift = lanes_of(term[slot], 0)
        label = lanes_of(labels[pb], 0) - first_class - own_at
        for n in range(queries // 256):
            at = slice(256 * n, 256 * n + 256)
            if slot < 2:
                inner = early[slot, :, at]
            else:
                inner = dot(protos[pl.ds(own_at, own_rows), :], qall[slot, at, :], NT)
            pn = pn_own[...]
            pn = jnp.concatenate([pn, pn], axis=1)
            g = jnp.exp(inner * (2.0 * factor) - pn - shift[:, at])
            index = lax.broadcasted_iota(jnp.int32, (own_rows, 256), 0)
            g = (g - jnp.where(index == label[:, at], 1.0, 0.0)).astype(jnp.bfloat16)
            gbuf[:, at] = g
            g32 = g.astype(jnp.float32)
            col = g32[:, 0:128] + g32[:, 128:256]
            if slot or n:
                coltot[...] += col
            else:
                coltot[...] = col

        @pl.loop(0, width // 256)
        def _(n):
            cols = pl.ds(pl.multiple_of(n * 256, 256), 256)
            moment = dot(gbuf[...], qall[slot, :, cols], NN)
            if slot:
                acc[:, cols] += moment
            else:
                acc[:, cols] = moment

    def x_done(h):
        rows = pl.ds(h * part, part)
        for d in (1, 3, 2):
            if h == 0:
                arrived(xrc.at[d - 1], xc_ssem.at[d - 1], xc_rsem.at[d - 1])
            arrived(xr.at[d - 1, rows], x_ssem.at[d - 1, h], x_rsem.at[d - 1, h])
        for n in range(NZ):
            cols = slice(128 * n, 128 * n + 128)
            v = own_x[rows, cols]
            for d in range(1, NX):
                v = v + xr[d - 1, rows, cols].astype(jnp.float32) * xrc[d - 1, n : n + 1, :]
            own_x[rows, cols] = v
            power, lines = coded(v)
            zs[h, n, 0:part, :] = lines
            zs[h, n, part : part + 16, :] = rows16(power)
        for d in (4, 3, 5, 2, 6, 1, 7):
            sent.append(send(zs.at[h, at_z(d)], zr.at[h, d], z_ssem.at[h, d], z_rsem.at[h, d], dev_z(d)))

    def z_done(h):
        for d in (1, 7, 2, 6, 3, 5, 4):
            arrived(zr.at[h, d], z_ssem.at[h, d], z_rsem.at[h, d])
        v = own_x[pl.ds(h * part, part), pl.ds(pl.multiple_of(z * 128, 128), 128)]
        for d in range(1, NZ):
            s = scale_of(zr[h, d, part : part + 16, :])[0:1]
            v = v + zr[h, d, 0:part, :].astype(jnp.float32) * s
        power, lines = coded(v * (2.0 * factor))
        gx[h, x, z, 0:part, :] = lines
        gx[h, x, z, part : part + 16, :] = rows16(power)
        for d in (4, 3, 5, 2, 6, 1, 7):
            sent.append(send(gx.at[h, x, z], gx.at[h, x, z], gz_ssem.at[h, d], gz_rsem.at[h, z], dev_z(d)))

    def gz_done(h):
        for d in (1, 7, 2, 6, 3, 5, 4):
            arrived(gx.at[h, x, at_z(d)], gz_ssem.at[h, d], gz_rsem.at[h, at_z(d)])
        gsc[h, x] = jnp.concatenate(
            [scale_of(gx[h, x, n, part : part + 16, :])[0:1] for n in range(NZ)], axis=0
        )
        for d in (2, 1, 3):
            sent.append(send(gsc.at[h, x], gsc.at[h, x], gc_ssem.at[h, d], gc_rsem.at[h, x], dev_x(d)))
            lines = gx.at[h, x, pl.ds(0, NZ), pl.ds(0, part)]
            sent.append(send(lines, lines, gx_ssem.at[h, d], gx_rsem.at[h, x], dev_x(d)))

    def gx_done(h):
        for d in (1, 3, 2):
            k = at_x(d)
            arrived(gsc.at[h, k], gc_ssem.at[h, d], gc_rsem.at[h, k])
            arrived(gx.at[h, k, pl.ds(0, NZ), pl.ds(0, part)], gx_ssem.at[h, d], gx_rsem.at[h, k])

    def to_other_core(slot, first):
        dy = SLOTS[slot][0]
        for k in range(2):
            q_send(slot, slot_at[dy, 1], halves[k], first + k, sibling)

    def relay():
        q_wait(slot_at[3, 0], halves[0], 0)
        q_send(slot_at[3, 0], slot_at[2, 0], halves[0], 4, up)
        q_wait(slot_at[1, 0], halves[1], 2)
        q_send(slot_at[1, 0], slot_at[2, 0], halves[1], 5, down)

    proto_block(0)
    x_done(0)
    relay()
    proto_block(1)
    x_done(1)
    q_wait(slot_at[3, 0], halves[1], 1)
    to_other_core(2, 8)
    q_wait(slot_at[1, 0], halves[0], 3)
    to_other_core(3, 10)
    z_done(0)
    proto_block(2)
    z_done(1)
    proto_block(3)
    gz_done(0)
    q_wait(4, halves[0], 8)
    q_wait(4, halves[1], 9)
    proto_block(4)
    gz_done(1)
    q_wait(5, halves[0], 10)
    q_wait(5, halves[1], 11)
    proto_block(5)
    q_wait(slot_at[2, 0], halves[0], 4)
    q_wait(slot_at[2, 0], halves[1], 5)
    to_other_core(6, 12)
    proto_block(6)
    q_wait(7, halves[0], 12)
    q_wait(7, halves[1], 13)
    proto_block(7)

    @pl.loop(0, own_rows // 128)
    def _(i):
        rows = pl.ds(pl.multiple_of(i * 128, 128), 128)
        own = protos[pl.ds(pl.multiple_of(own_at + i * 128, 128), 128), :].astype(jnp.float32)
        total = jnp.sum(coltot[rows, :], axis=1, keepdims=True)
        pg_out[rows, :] = (2.0 * factor) * (acc[rows, :] - total * own)

    late = 2 * PARTS * (NX - 1)
    for copy in sent[:-late]:
        copy.wait_send()
    for h in range(PARTS):
        gx_done(h)
    for copy in sent[-late:]:
        copy.wait_send()
    pltpu.make_async_remote_copy(
        src_ref=stat.at[pl.ds(0, group - 1)], dst_ref=stat.at[pl.ds(0, group - 1)],
        send_sem=st_ssem, recv_sem=st_rsem, device_id=(ci, pi), device_id_type=MESH,
    ).wait_send()


def finish(stats, gx, gsc, pg, loss_out, qg_out, pg_out, loss, lines, sem):
    part = gx.shape[3] - 16
    block = PARTS * part
    copies = [pltpu.make_async_copy(pg, pg_out, sem.at[NX])]
    loss[...] = stats[0:4] - stats[4:8]
    copies.append(pltpu.make_async_copy(loss, loss_out, sem.at[NX + 1]))
    for copy in copies:
        copy.start()
    for k in range(NX):
        for h in range(PARTS):
            at = k * block + h * part
            for n in range(NZ):
                value = gx[h, k, n, 0:part, :].astype(jnp.float32) * gsc[h, k, n : n + 1, :]
                lines[at : at + part, 128 * n : 128 * n + 128] = value
        rows = pl.ds(k * block, block)
        copies.append(pltpu.make_async_copy(lines.at[rows], qg_out.at[rows], sem.at[k]))
        copies[-1].start()
    for copy in copies:
        copy.wait()


def local(queries, labels, prototypes):
    rows, width = queries.shape
    classes = prototypes.shape[0]
    own_rows = classes // (2 * NY)
    block = rows // NX
    part = block // PARTS
    vmem = pltpu.VMEM
    dma = pltpu.SemaphoreType.DMA
    f32, bf16, i16 = jnp.float32, jnp.bfloat16, jnp.int16
    sent_block = (PARTS, NX, NZ, part + 16, 128)
    scratch = [
        vmem((2 * NY, 4, rows // 4), jnp.int32),
        vmem((classes, width), bf16),
        vmem((2 * NY, rows, width), bf16),
        [vmem((rows, 1024), f32)] * 2,
        [vmem((rows, 1024), f32)] * (classes // 1024),
        vmem((rows, classes), bf16),
        vmem((8, classes), f32),
        vmem((block, width), f32),
        vmem((NX * NZ, 8, 128), f32),
        vmem((2 * NY, 8, 128), f32),
        vmem((8, rows), f32),
        vmem((rows, 128), jnp.int32),
        vmem((classes // 1024, rows, 128), f32),
        vmem((classes // 1024, rows, 128), f32),
        vmem((rows, 128), f32),
        vmem((NX - 1, block, width), i16),
        vmem((NX - 1, block, width), i16),
        vmem((NX - 1, 8, 128), f32),
        vmem((NX - 1, 8, 128), f32),
        vmem((PARTS, NZ, part + 16, 128), i16),
        vmem((PARTS, NZ, part + 16, 128), i16),
        vmem((own_rows, width), f32),
        vmem((own_rows, 128), f32),
        vmem((own_rows, 128), f32),
        vmem((own_rows, rows), bf16),
        vmem((2, own_rows, rows), f32),
        dma((classes // 256 + 2,)),
        dma((14,)), dma((14,)),
        dma(()), dma(()),
        dma((8,)), dma((8,)),
        dma((NX - 1, PARTS)), dma((NX - 1, PARTS)),
        dma((NX - 1,)), dma((NX - 1,)),
        dma((PARTS, NZ)), dma((PARTS, NZ)),
        dma((PARTS, NZ)), dma((PARTS, NZ)),
        dma((PARTS, NX)), dma((PARTS, NX)),
        dma((PARTS, NX)), dma((PARTS, NX)),
    ]
    here = pl.BlockSpec(memory_space=pltpu.VMEM)
    anywhere = pl.BlockSpec(memory_space=pl.ANY)
    stats, gx, gsc, pg = pl.pallas_call(
        kernel,
        out_shape=(
            jax.ShapeDtypeStruct((8, 128), f32),
            jax.ShapeDtypeStruct(sent_block, i16),
            jax.ShapeDtypeStruct((PARTS, NX, NZ, 128), f32),
            jax.ShapeDtypeStruct((own_rows, width), f32),
        ),
        in_specs=[pl.BlockSpec(memory_space=pltpu.HBM)] * 3,
        out_specs=[here] * 4,
        scratch_shapes=scratch,
        compiler_params=pltpu.CompilerParams(
            collective_id=0, has_side_effects=True, vmem_limit_bytes=48 * 2**20
        ),
    )(queries, labels.reshape(2 * NY, 4, rows // 4), prototypes)
    loss, query_grad, proto_grad = pl.pallas_call(
        finish,
        out_shape=(
            jax.ShapeDtypeStruct((4, rows // 4), f32),
            jax.ShapeDtypeStruct((rows, width), f32),
            jax.ShapeDtypeStruct((own_rows, width), f32),
        ),
        in_specs=[here] * 4,
        out_specs=[anywhere] * 3,
        scratch_shapes=[vmem((4, rows // 4), f32), vmem((rows, width), f32), dma((NX + 2,))],
        compiler_params=pltpu.CompilerParams(vmem_limit_bytes=8 * 2**20),
    )(stats, gx, gsc, pg)
    return loss.reshape(rows), query_grad, proto_grad


def solution(mesh):
    placed = (P("pb", None), P(), P("cls", None))
    return jax.shard_map(
        local,
        mesh=mesh,
        in_specs=placed,
        out_specs=(P("pb"), P("pb", None), P(("cls", "pb"), None)),
        check_vma=False,
    )
```
